1024 devices in a mesh: row: 16 (over x_hi, y, core), pitch: 32 (over z), span: 2 (over x_lo).
Axes of the slice: x: 4 (x_hi: 2, x_lo: 2; x = x_hi * 2 + x_lo), y: 4, z: 32, core: 2. Of those that a mesh axis runs over, the one named last changes fastest.
Arguments:
- outlet: bfloat16 [16, 2, 5, 1024, 4096], P('row', None, None, 'span', 'pitch'), may hold values from -6 to 6
- remap_weight: bfloat16 [1024, 896], P('span'), may hold values from -0.4375 to 0.4375
- band_start: int32 [896], replicated, may hold values from 0 to 832, as said below
- blade_counts: int32 [2], replicated, may hold values from 12 to 60
- mode_orders: int32 [64, 2], replicated, may hold values from -4 to 4
Outputs:
- stator_inlet: bfloat16 [16, 2, 5, 896, 4096], P('row', None, None, 'span', 'pitch')
The draws below stay inside these ranges and needn't reach their ends.
Inputs may be any that keep to these rules, and one draw needn't show every extreme that they name: Stator radial row m draws from rotor radial rows band_start[m] to band_start[m] + 191; band_start[m] lies within 6 rows of m * 832 / 895, band_start[0] = 0 and band_start[895] = 832.
All inputs are finite; a program needn't handle non-finite values.
Results may differ from the reference program's by a relative error of at most 0.0068.
Values may be sent and summed in bfloat16 or wider, within the bound.
A program may use at most 32 MiB of HBM per device.

```python
import math
import jax
import jax.numpy as jnp
from jax import lax

R = 1024
RS = 896
PITCH = 4096
HARM = 64
FIELDS = 5
BAND = 192
INST_DEV = 2
ROWS = 16
NTIME = 32


def draw_band_start(key, part):
    stator_rows = jnp.arange(RS, dtype=jnp.int32)
    centred = stator_rows * (R - BAND) // (RS - 1)
    jitter = jax.random.randint(key, (RS,), -6, 7, dtype=jnp.int32)
    starts = jnp.clip(centred + jitter, 0, R - BAND)
    starts = jnp.where(stator_rows == 0, 0, jnp.where(stator_rows == RS - 1, R - BAND, starts))
    return starts.astype(jnp.int32)


def with_ends(array, rng, low, top_value):
    longest = array.shape.index(max(array.shape))
    spots = []
    for shift in (0, 1):
        where = [jax.random.randint(jax.random.fold_in(rng, axis), (), 0, length) for axis, length in enumerate(array.shape)]
        where[longest] = (where[longest] + shift) % array.shape[longest]
        spots.append(tuple(where))
    return array.at[spots[0]].set(low).at[spots[1]].set(top_value)


def steps_of(key, extent, shards, least, top_value):
    level = 1.0
    for dim, blocks in shards:
        heights = jax.random.uniform(jax.random.fold_in(jax.random.fold_in(key, 6), dim), (blocks,), jnp.float32, least / len(shards), top_value / len(shards))
        level = level * jnp.repeat(jnp.exp(heights), extent[dim] // blocks).reshape((-1,) + (1,) * (len(extent) - 1 - dim))
    return level


def bell_draw(stream_key, shape, scale, limit, cuts=(), held_as=jnp.bfloat16):
    drawn = jax.random.normal(stream_key, shape, jnp.float32) * scale
    if len(cuts) > 0:
        drawn = steps_of(stream_key, shape, cuts, -0.22, 0.18) * drawn
    return jnp.clip(drawn, min=-limit, max=limit).astype(held_as)


def setup_inputs(seed: int = 0) -> dict:
    key_list = jax.random.split(jax.random.key(seed), 6)
    return {
        "outlet": bell_draw(key_list[0], (ROWS, INST_DEV, FIELDS, R, PITCH), 1.0, 6.0, ((0, 16), (3, 2), (4, 32))),
        "remap_weight": bell_draw(key_list[1], (R, RS), BAND ** -0.5, 0.4375, ((0, 2),)),
        "band_start": draw_band_start(jax.random.fold_in(key_list[5], 71), 0),
        "blade_counts": jax.random.randint(key_list[3], (2,), 12, 61).astype(jnp.int32),
        "mode_orders": with_ends(jax.random.randint(key_list[4], (HARM, 2), -4, 5), jax.random.fold_in(key_list[4], 1), -4, 4).astype(jnp.int32),
    }


def pitch_table(wavenumber, first_row, number, total_pitch):
    circumferential_coordinates = first_row + jnp.arange(number, dtype=jnp.int32)
    angular_offsets = jnp.mod(circumferential_coordinates[:, None] * wavenumber[None, :], total_pitch)
    angles = 2.0 * math.pi / total_pitch * angular_offsets.astype(jnp.float32)
    return jnp.stack([jnp.cos(angles), jnp.sin(angles)], axis=2).reshape(number, 2 * wavenumber.shape[0])

def reference(outlet, remap_weight, band_start, blade_counts, mode_orders):
    wavenumber = mode_orders[:, 0] * blade_counts[0] + mode_orders[:, 1] * blade_counts[1]
    raw_table = pitch_table(wavenumber, 0, PITCH, PITCH)
    analysis = (raw_table * math.sqrt(2.0 / PITCH)).astype(jnp.bfloat16)
    synthesis = (raw_table * (1.0 / math.sqrt(HARM))).astype(jnp.bfloat16)
    radial_rows = jnp.arange(R, dtype=jnp.int32)
    in_band = (radial_rows[:, None] >= band_start[None, :]) & (radial_rows[:, None] < band_start[None, :] + BAND)
    banded_t = jnp.where(in_band, remap_weight, jnp.zeros_like(remap_weight)).T
    vane_passing_interval = NTIME * blade_counts[0]

    def single_plane(plane_index):
        target_row = plane_index // INST_DEV
        within = plane_index % INST_DEV
        source_row = (target_row + ROWS // 2) % ROWS
        slab_plane = lax.dynamic_index_in_dim(lax.dynamic_index_in_dim(outlet, source_row, 0, False), within, 0, False)
        moment_value = source_row * INST_DEV + within
        spectra = jnp.dot(slab_plane.reshape(FIELDS * R, PITCH), analysis, preferred_element_type=jnp.float32)
        angular_offsets = jnp.mod(wavenumber * moment_value, vane_passing_interval)
        angles = 2.0 * math.pi * angular_offsets.astype(jnp.float32) / vane_passing_interval.astype(jnp.float32)
        cosine = jnp.cos(angles)
        sine_part = jnp.sin(angles)
        paired = spectra.reshape(FIELDS * R, HARM, 2)
        cos_part = paired[:, :, 0]
        sin_part = paired[:, :, 1]
        rotated = jnp.stack([cos_part * cosine - sin_part * sine_part, cos_part * sine_part + sin_part * cosine], axis=2)
        rotated = rotated.reshape(FIELDS, R, 2 * HARM).astype(jnp.bfloat16)
        by_radius = jnp.transpose(rotated, (1, 0, 2)).reshape(R, FIELDS * 2 * HARM)
        remapped = jnp.dot(banded_t, by_radius, preferred_element_type=jnp.float32).astype(jnp.bfloat16)
        by_field = jnp.transpose(remapped.reshape(RS, FIELDS, 2 * HARM), (1, 0, 2)).reshape(FIELDS * RS, 2 * HARM)
        inlet_rows = jnp.dot(by_field, synthesis.T, preferred_element_type=jnp.float32).astype(jnp.bfloat16)
        return inlet_rows.reshape(FIELDS, RS, PITCH)
    results = lax.map(single_plane, jnp.arange(ROWS * INST_DEV, dtype=jnp.int32))
    return results.reshape(ROWS, INST_DEV, FIELDS, RS, PITCH)
```

```python
import functools
import math

import jax
import jax.numpy as jnp
from jax import lax
from jax.experimental import pallas as pl
from jax.experimental.pallas import tpu as pltpu
from jax.sharding import PartitionSpec as P

BAND = 192
MESH = pl.DeviceIdType.MESH
F32 = jnp.float32
BF16 = jnp.bfloat16


def nt_dot(a, b):
    return lax.dot_general(a, b, (((1,), (1,)), ((), ())), preferred_element_type=F32)


def nn_dot(a, b):
    return lax.dot_general(a, b, (((1,), (0,)), ((), ())), preferred_element_type=F32)


def kernel(
    n, rows_n, chunk, subs, halo, half,
    x_ref, own_ref, cross_ref, ana_ref, syn_ref, rot_ref, out_ref,
    part, xsend, xrecv, sb_r, rb_r, sb_l, rb_l, fin, gath, outv,
    s_sr, s_rr, s_sl, s_rl, s_xs, s_xr, s_hs, s_hr, a_sr, a_rr, a_sl, a_rl, s_out,
):
    planes, rad, _ = x_ref.shape
    srows = own_ref.shape[0]
    width = cross_ref.shape[1]
    sub = chunk // subs
    z = lax.axis_index("pitch")
    g = lax.axis_index("row")
    h = lax.axis_index("span")
    right = lax.rem(z + 1, n)
    left = lax.rem(z + n - 1, n)
    other = 1 - h
    partner = lax.rem(g + rows_n // 2, rows_n)
    hops_r = n // 2
    hops_l = n - 1 - hops_r

    barrier = pltpu.get_barrier_semaphore()
    for where in ({"pitch": left}, {"pitch": right}, {"span": other}, {"row": partner}):
        pl.semaphore_signal(barrier, inc=1, device_id=where, device_id_type=MESH)

    cols0 = (rad - width) * (1 - h)
    def cross_plane(k, c):
        xk = x_ref[k, pl.ds(pl.multiple_of(cols0, 128), width), :]
        xsend[k] = nn_dot(cross_ref[...], xk).astype(BF16)
        return c
    lax.fori_loop(0, planes, cross_plane, 0)

    pl.semaphore_wait(barrier, 4)
    xcopy = pltpu.make_async_remote_copy(
        src_ref=xsend, dst_ref=xrecv, send_sem=s_xs, recv_sem=s_xr,
        device_id={"span": other}, device_id_type=MESH)
    xcopy.start()

    ana = ana_ref[...]
    def own_plane(k, c):
        mk = nn_dot(own_ref[...], x_ref[k]).astype(BF16)
        part[pl.ds(pl.multiple_of(k * srows, 16), srows), :] = nt_dot(mk, ana)
        return c
    lax.fori_loop(0, planes, own_plane, 0)
    tail = part.shape[0] - planes * srows
    if tail:
        part[planes * srows:, :] = jnp.zeros((tail, part.shape[1]), F32)
    xcopy.wait_recv()
    b0 = (srows - halo) * (1 - h)
    def add_plane(k, c):
        at = pl.ds(pl.multiple_of(k * srows + b0, 16), halo)
        part[at, :] = part[at, :] + nt_dot(xrecv[k], ana)
        return c
    lax.fori_loop(0, planes, add_plane, 0)

    def rows_of(c, j):
        return pl.ds(pl.multiple_of(c * chunk + j * sub, 16), sub)

    def send_r(s, j):
        return pltpu.make_async_remote_copy(
            src_ref=sb_r.at[s, j], dst_ref=rb_r.at[s, j], send_sem=s_sr.at[s, j], recv_sem=s_rr.at[s, j],
            device_id={"pitch": right}, device_id_type=MESH)

    def send_l(s, j):
        return pltpu.make_async_remote_copy(
            src_ref=sb_l.at[s, j], dst_ref=rb_l.at[s, j], send_sem=s_sl.at[s, j], recv_sem=s_rl.at[s, j],
            device_id={"pitch": left}, device_id_type=MESH)

    def chunk_r(s):
        return lax.rem(z + hops_r - s + n, n)

    def chunk_l(s):
        return lax.rem(z - hops_l + s + n, n)

    for j in range(subs):
        sb_r[0, j] = part[rows_of(chunk_r(0), j), :].astype(BF16)
        send_r(0, j).start()
        sb_l[0, j] = part[rows_of(chunk_l(0), j), :].astype(BF16)
        send_l(0, j).start()

    def step(s, c):
        for j in range(subs):
            send_r(s - 1, j).wait_recv()
            sb_r[s, j] = (part[rows_of(chunk_r(s), j), :] + rb_r[s - 1, j].astype(F32)).astype(BF16)
            send_r(s, j).start()
            send_l(s - 1, j).wait_recv()
            sb_l[s, j] = (part[rows_of(chunk_l(s), j), :] + rb_l[s - 1, j].astype(F32)).astype(BF16)
            send_l(s, j).start()
        return c
    lax.fori_loop(1, hops_l, step, 0)
    for s in range(hops_l, hops_r):
        for j in range(subs):
            send_r(s - 1, j).wait_recv()
            sb_r[s, j] = (part[rows_of(chunk_r(s), j), :] + rb_r[s - 1, j].astype(F32)).astype(BF16)
            send_r(s, j).start()

    cut = half * srows

    def hop(j):
        return pltpu.make_async_remote_copy(
            src_ref=fin.at[j], dst_ref=gath.at[z, j], send_sem=s_hs.at[j], recv_sem=s_hr.at[j],
            device_id={"row": partner}, device_id_type=MESH)

    for j in range(subs):
        send_l(hops_l - 1, j).wait_recv()
        total = part[rows_of(z, j), :] + rb_l[hops_l - 1, j].astype(F32)
        send_r(hops_r - 1, j).wait_recv()
        total = total + rb_r[hops_r - 1, j].astype(F32)
        at = z * chunk + j * sub + lax.broadcasted_iota(jnp.int32, total.shape, 0)
        first = at < cut
        cosine = jnp.where(first, rot_ref[0:1, :], rot_ref[1:2, :])
        sine = jnp.where(first, rot_ref[2:3, :], rot_ref[3:4, :])
        swapped = pltpu.roll(total, total.shape[1] // 2, 1)
        fin[j] = (total * cosine + swapped * sine).astype(BF16)
        hop(j).start()

    def fwd_r(s, j):
        at = gath.at[lax.rem(z - s + n, n), j]
        return pltpu.make_async_remote_copy(
            src_ref=at, dst_ref=at, send_sem=a_sr.at[s, j], recv_sem=a_rr.at[s, j],
            device_id={"pitch": right}, device_id_type=MESH)

    def fwd_l(s, j):
        at = gath.at[lax.rem(z + s, n), j]
        return pltpu.make_async_remote_copy(
            src_ref=at, dst_ref=at, send_sem=a_sl.at[s, j], recv_sem=a_rl.at[s, j],
            device_id={"pitch": left}, device_id_type=MESH)

    def recv_r(s, j):
        at = gath.at[lax.rem(z - s - 1 + n, n), j]
        return pltpu.make_async_remote_copy(
            src_ref=at, dst_ref=at, send_sem=a_sr.at[s, j], recv_sem=a_rr.at[s, j],
            device_id={"pitch": right}, device_id_type=MESH)

    def recv_l(s, j):
        at = gath.at[lax.rem(z + s + 1, n), j]
        return pltpu.make_async_remote_copy(
            src_ref=at, dst_ref=at, send_sem=a_sl.at[s, j], recv_sem=a_rl.at[s, j],
            device_id={"pitch": left}, device_id_type=MESH)

    syn = syn_ref[...]

    def emit(c, j):
        outv[rows_of(c, j), :] = nn_dot(gath[c, j], syn).astype(BF16)

    for j in range(subs):
        hop(j).wait_recv()
        fwd_r(0, j).start()
        fwd_l(0, j).start()
    for j in range(subs):
        emit(z, j)

    def ag_step(s, c):
        for j in range(subs):
            recv_r(s - 1, j).wait_recv()
            fwd_r(s, j).start()
            recv_l(s - 1, j).wait_recv()
            fwd_l(s, j).start()
        for j in range(subs):
            emit(lax.rem(z - s + n, n), j)
            emit(lax.rem(z + s, n), j)
        return c
    lax.fori_loop(1, hops_l, ag_step, 0)
    for s in range(hops_l, hops_r):
        for j in range(subs):
            recv_r(s - 1, j).wait_recv()
            fwd_r(s, j).start()
        for j in range(subs):
            emit(lax.rem(z - s + n, n), j)
    for j in range(subs):
        recv_l(hops_l - 1, j).wait_recv()
        emit(lax.rem(z + hops_l, n), j)
    for j in range(subs):
        recv_r(hops_r - 1, j).wait_recv()
        emit(lax.rem(z - hops_r + n, n), j)

    done = pltpu.make_async_copy(outv.at[pl.ds(0, planes * srows)], out_ref, s_out)
    done.start()

    xcopy.wait_send()
    for j in range(subs):
        hop(j).wait_send()

    def drain_r(s, c):
        for j in range(subs):
            send_r(s, j).wait_send()
            fwd_r(s, j).wait_send()
        return c
    lax.fori_loop(0, hops_r, drain_r, 0)

    def drain_l(s, c):
        for j in range(subs):
            send_l(s, j).wait_send()
            fwd_l(s, j).wait_send()
        return c
    lax.fori_loop(0, hops_l, drain_l, 0)
    done.wait()


def body(outlet, remap_weight, band_start, blade_counts, mode_orders):
    row_count = lax.axis_size("row")
    n = lax.axis_size("pitch")
    g = lax.axis_index("row")
    z = lax.axis_index("pitch")
    h = lax.axis_index("span")
    planes = outlet[0]
    inst, fields, rad, pitch = planes.shape
    total_pitch = pitch * n
    harm = mode_orders.shape[0]
    cols = 2 * harm
    stator = remap_weight.shape[1]
    srows = stator // 2
    nplanes = inst * fields
    wave = mode_orders[:, 0] * blade_counts[0] + mode_orders[:, 1] * blade_counts[1]

    place = z * pitch + jnp.arange(pitch, dtype=jnp.int32)
    q = jnp.mod(place[None, :] * wave[:, None], total_pitch)
    ang = 2.0 * math.pi / total_pitch * q.astype(F32)
    table = jnp.concatenate([jnp.cos(ang), jnp.sin(ang)], axis=0)
    ana = (table * math.sqrt(2.0 / total_pitch)).astype(BF16)
    syn = (table * (1.0 / math.sqrt(harm))).astype(BF16)

    moments = g * inst + jnp.arange(inst, dtype=jnp.int32)
    period = row_count * inst * blade_counts[0]
    turn = jnp.mod(wave[None, :] * moments[:, None], period)
    theta = 2.0 * math.pi * turn.astype(F32) / period.astype(F32)
    co, si = jnp.cos(theta), jnp.sin(theta)
    rot = jnp.concatenate(
        [jnp.concatenate([co, co], 1), jnp.concatenate([-si, si], 1), jnp.zeros((8 - 2 * inst, cols), F32)], 0)

    rows = h * rad + jnp.arange(rad, dtype=jnp.int32)
    inb = (rows[:, None] >= band_start[None, :]) & (rows[:, None] < band_start[None, :] + BAND)
    banded = jnp.where(inb, remap_weight, jnp.zeros_like(remap_weight)).T
    halo, width = 112, 128
    own = lax.dynamic_slice_in_dim(banded, h * srows, srows, 0)
    cross = lax.dynamic_slice(banded, (srows - halo * h, (rad - width) * (1 - h)), (halo, width))

    nrows = nplanes * srows
    chunk = -(-nrows // (n * 16)) * 16
    subs = 3 if chunk % 48 == 0 else (2 if chunk % 32 == 0 else 1)
    sub = chunk // subs
    hr, hl = n // 2, n - 1 - n // 2
    vm = pl.BlockSpec(memory_space=pltpu.VMEM)
    out = pl.pallas_call(
        functools.partial(kernel, n, row_count, chunk, subs, halo, fields),
        out_shape=jax.ShapeDtypeStruct((nrows, pitch), BF16),
        in_specs=[vm] * 6,
        out_specs=pl.BlockSpec(memory_space=pl.ANY),
        scratch_shapes=[
            pltpu.VMEM((n * chunk, cols), F32),
            pltpu.VMEM((nplanes, halo, pitch), BF16),
            pltpu.VMEM((nplanes, halo, pitch), BF16),
            pltpu.VMEM((hr, subs, sub, cols), BF16),
            pltpu.VMEM((hr, subs, sub, cols), BF16),
            pltpu.VMEM((hl, subs, sub, cols), BF16),
            pltpu.VMEM((hl, subs, sub, cols), BF16),
            pltpu.VMEM((subs, sub, cols), BF16),
            pltpu.VMEM((n, subs, sub, cols), BF16),
            pltpu.VMEM((n * chunk, pitch), BF16),
            pltpu.SemaphoreType.DMA((hr, subs)),
            pltpu.SemaphoreType.DMA((hr, subs)),
            pltpu.SemaphoreType.DMA((hl, subs)),
            pltpu.SemaphoreType.DMA((hl, subs)),
            pltpu.SemaphoreType.DMA,
            pltpu.SemaphoreType.DMA,
            pltpu.SemaphoreType.DMA((subs,)),
            pltpu.SemaphoreType.DMA((subs,)),
            pltpu.SemaphoreType.DMA((hr, subs)),
            pltpu.SemaphoreType.DMA((hr, subs)),
            pltpu.SemaphoreType.DMA((hl, subs)),
            pltpu.SemaphoreType.DMA((hl, subs)),
            pltpu.SemaphoreType.DMA,
        ],
        compiler_params=pltpu.CompilerParams(
            collective_id=0, has_side_effects=True, vmem_limit_bytes=40 * 1024 * 1024),
    )(planes.reshape(nplanes, rad, pitch), own, cross, ana, syn, rot)
    return out.reshape(1, inst, fields, srows, pitch)


def solution(mesh):
    placed = (P("row", None, None, "span", "pitch"), P("span", None), P(), P(), P())
    return jax.shard_map(
        body, mesh=mesh, in_specs=placed,
        out_specs=P("row", None, None, "span", "pitch"), check_vma=False)
```

```python
import functools
import math

import jax
import jax.numpy as jnp
from jax import lax
from jax.experimental import pallas as pl
from jax.experimental.pallas import tpu as pltpu
from jax.sharding import PartitionSpec as P

BAND = 192
MESH = pl.DeviceIdType.MESH
F32 = jnp.float32
BF16 = jnp.bfloat16


def nt_dot(a, b):
    return lax.dot_general(a, b, (((1,), (1,)), ((), ())), preferred_element_type=F32)


def nn_dot(a, b):
    return lax.dot_general(a, b, (((1,), (0,)), ((), ())), preferred_element_type=F32)


def kernel(
    n, rows_n, chunk, halo, half,
    x_ref, own_ref, cross_ref, ana_ref, syn_ref, rot_ref, out_ref,
    part, xsend, xrecv, sb_r, rb_r, sb_l, rb_l, sums, from_roots, gath,
    s_sr, s_rr, s_sl, s_rl, s_xs, s_xr, e_s, e_r, g_s, g_r, a_sr, a_rr, a_sl, a_rl,
):
    planes, rad, _ = x_ref.shape
    srows = own_ref.shape[0]
    width = cross_ref.shape[1]
    reach = (n - 2) // 6
    far = 2 * reach + 1
    z = lax.axis_index("pitch")
    g = lax.axis_index("row")
    h = lax.axis_index("span")
    other = 1 - h
    partner = lax.rem(g + rows_n // 2, rows_n)

    def at(d):
        return lax.rem(z + (d + n), n)

    right, left = at(1), at(-1)
    offsets = (far, -far, 0)

    barrier = pltpu.get_barrier_semaphore()
    peers = [{"pitch": left}, {"pitch": right}, {"span": other}]
    peers += [{"pitch": at(far)}, {"pitch": at(-far)}]
    peers += [{"row": partner, "pitch": at(d)} for d in offsets]
    for where in peers:
        pl.semaphore_signal(barrier, inc=1, device_id=where, device_id_type=MESH)

    cols0 = (rad - width) * (1 - h)

    def cross_plane(k, c):
        xk = x_ref[k, pl.ds(pl.multiple_of(cols0, 128), width), :]
        xsend[k] = nn_dot(cross_ref[...], xk).astype(BF16)
        return c

    lax.fori_loop(0, planes, cross_plane, 0)

    pl.semaphore_wait(barrier, len(peers))

    def remote(src, dst, send, recv, where):
        return pltpu.make_async_remote_copy(
            src_ref=src, dst_ref=dst, send_sem=send, recv_sem=recv, device_id=where, device_id_type=MESH
        )

    xcopy = remote(xsend, xrecv, s_xs, s_xr, {"span": other})
    xcopy.start()

    ana = ana_ref[...]

    def own_plane(k, c):
        mk = nn_dot(own_ref[...], x_ref[k]).astype(BF16)
        part[pl.ds(pl.multiple_of(k * srows, 16), srows), :] = nt_dot(mk, ana)
        return c

    lax.fori_loop(0, planes, own_plane, 0)
    tail = part.shape[0] - planes * srows
    if tail:
        part[planes * srows :, :] = jnp.zeros((tail, part.shape[1]), F32)
    xcopy.wait_recv()
    b0 = (srows - halo) * (1 - h)

    def add_plane(k, c):
        rows = pl.ds(pl.multiple_of(k * srows + b0, 16), halo)
        part[rows, :] = part[rows, :] + nt_dot(xrecv[k], ana)
        return c

    lax.fori_loop(0, planes, add_plane, 0)

    def rows_of(c):
        return pl.ds(pl.multiple_of(c * chunk, 16), chunk)

    def send_r(s, k):
        return remote(sb_r.at[s, k], rb_r.at[s, k], s_sr.at[s, k], s_rr.at[s, k], {"pitch": right})

    def send_l(s, k):
        return remote(sb_l.at[s, k], rb_l.at[s, k], s_sl.at[s, k], s_rl.at[s, k], {"pitch": left})

    def first_r(k):
        return 1 if k == 1 else 0

    for s in range(reach):
        for k, off in enumerate(offsets):
            if s >= first_r(k):
                value = part[rows_of(at(reach - s - off)), :]
                if s > first_r(k):
                    send_r(s - 1, k).wait_recv()
                    value = value + rb_r[s - 1, k].astype(F32)
                sb_r[s, k] = value.astype(BF16)
                send_r(s, k).start()
            value = part[rows_of(at(s - reach - off)), :]
            if s > 0:
                send_l(s - 1, k).wait_recv()
                value = value + rb_l[s - 1, k].astype(F32)
            sb_l[s, k] = value.astype(BF16)
            send_l(s, k).start()

    def to_owner(k):
        where = {"row": partner, "pitch": at(-offsets[k])}
        return remote(sums.at[k], from_roots.at[k], e_s.at[k], e_r.at[k], where)

    for k, off in enumerate(offsets):
        value = part[rows_of(at(-off)), :]
        send_l(reach - 1, k).wait_recv()
        value = value + rb_l[reach - 1, k].astype(F32)
        if reach - 1 >= first_r(k):
            send_r(reach - 1, k).wait_recv()
            value = value + rb_r[reach - 1, k].astype(F32)
        sums[k] = value.astype(BF16)
        to_owner(k).start()

    for k in range(3):
        to_owner(k).wait_recv()
    total = from_roots[2].astype(F32) + from_roots[0].astype(F32) + from_roots[1].astype(F32)
    place = z * chunk + lax.broadcasted_iota(jnp.int32, total.shape, 0)
    first = place < half * srows
    cosine = jnp.where(first, rot_ref[0:1, :], rot_ref[1:2, :])
    sine = jnp.where(first, rot_ref[2:3, :], rot_ref[3:4, :])
    swapped = pltpu.roll(total, total.shape[1] // 2, 1)
    gath[z] = (total * cosine + swapped * sine).astype(BF16)

    def to_root(k, incoming=False):
        c = gath.at[at(-offsets[k])] if incoming else gath.at[z]
        return remote(c, c, g_s.at[k], g_r.at[k], {"pitch": at(offsets[k])})

    def fwd_r(s, k, incoming=False):
        c = gath.at[at(-s - (1 if incoming else 0) - offsets[k])]
        return remote(c, c, a_sr.at[s, k], a_rr.at[s, k], {"pitch": right})

    def fwd_l(s, k, incoming=False):
        c = gath.at[at(s + (1 if incoming else 0) - offsets[k])]
        return remote(c, c, a_sl.at[s, k], a_rl.at[s, k], {"pitch": left})

    def last_l(k):
        return reach - 2 if k == 1 else reach - 1

    syn = syn_ref[...]

    def emit(c):
        out_ref[rows_of(c), :] = nn_dot(gath[c], syn).astype(BF16)

    to_root(0).start()
    to_root(1).start()
    fwd_r(0, 2).start()
    fwd_l(0, 2).start()
    emit(z)

    def take(k, s):
        ready = []
        if s == 0:
            to_root(k, True).wait_recv()
            fwd_r(0, k).start()
            if last_l(k) >= 0:
                fwd_l(0, k).start()
            ready.append(at(-offsets[k]))
        else:
            fwd_r(s - 1, k, True).wait_recv()
            if s < reach:
                fwd_r(s, k).start()
            ready.append(at(-s - offsets[k]))
            if s - 1 <= last_l(k):
                fwd_l(s - 1, k, True).wait_recv()
                if s <= last_l(k):
                    fwd_l(s, k).start()
                ready.append(at(s - offsets[k]))
        return ready

    lag = min(3, reach)
    for t in range(1, reach + lag + 1):
        ready = []
        if t <= reach:
            ready += take(2, t)
        if t >= lag:
            ready += take(0, t - lag)
            ready += take(1, t - lag)
        for c in ready:
            emit(c)

    xcopy.wait_send()
    for k in range(3):
        to_owner(k).wait_send()
        if k < 2:
            to_root(k).wait_send()
        for s in range(reach):
            if s >= first_r(k):
                send_r(s, k).wait_send()
            send_l(s, k).wait_send()
            fwd_r(s, k).wait_send()
            if s <= last_l(k):
                fwd_l(s, k).wait_send()


def body(outlet, remap_weight, band_start, blade_counts, mode_orders):
    row_count = lax.axis_size("row")
    n = lax.axis_size("pitch")
    g = lax.axis_index("row")
    z = lax.axis_index("pitch")
    h = lax.axis_index("span")
    planes = outlet[0]
    inst, fields, rad, pitch = planes.shape
    total_pitch = pitch * n
    harm = mode_orders.shape[0]
    cols = 2 * harm
    stator = remap_weight.shape[1]
    srows = stator // 2
    nplanes = inst * fields
    wave = mode_orders[:, 0] * blade_counts[0] + mode_orders[:, 1] * blade_counts[1]

    place = z * pitch + jnp.arange(pitch, dtype=jnp.int32)
    q = jnp.mod(place[None, :] * wave[:, None], total_pitch)
    ang = 2.0 * math.pi / total_pitch * q.astype(F32)
    table = jnp.concatenate([jnp.cos(ang), jnp.sin(ang)], axis=0)
    ana = (table * math.sqrt(2.0 / total_pitch)).astype(BF16)
    syn = (table * (1.0 / math.sqrt(harm))).astype(BF16)

    moments = lax.rem(g + row_count // 2, row_count) * inst + jnp.arange(inst, dtype=jnp.int32)
    period = row_count * inst * blade_counts[0]
    turn = jnp.mod(wave[None, :] * moments[:, None], period)
    theta = 2.0 * math.pi * turn.astype(F32) / period.astype(F32)
    co, si = jnp.cos(theta), jnp.sin(theta)
    rot = jnp.concatenate(
        [jnp.concatenate([co, co], 1), jnp.concatenate([-si, si], 1), jnp.zeros((8 - 2 * inst, cols), F32)], 0)

    rows = h * rad + jnp.arange(rad, dtype=jnp.int32)
    inb = (rows[:, None] >= band_start[None, :]) & (rows[:, None] < band_start[None, :] + BAND)
    banded = jnp.where(inb, remap_weight, jnp.zeros_like(remap_weight)).T
    halo, width = 112, 128
    own = lax.dynamic_slice_in_dim(banded, h * srows, srows, 0)
    cross = lax.dynamic_slice(banded, (srows - halo * h, (rad - width) * (1 - h)), (halo, width))

    nrows = nplanes * srows
    chunk = -(-nrows // (n * 16)) * 16
    reach = (n - 2) // 6
    sem = pltpu.SemaphoreType.DMA
    vm = pl.BlockSpec(memory_space=pltpu.VMEM)
    out = pl.pallas_call(
        functools.partial(kernel, n, row_count, chunk, halo, fields),
        out_shape=jax.ShapeDtypeStruct((n * chunk, pitch), BF16),
        in_specs=[vm] * 6,
        out_specs=vm,
        scratch_shapes=[
            pltpu.VMEM((n * chunk, cols), F32),
            pltpu.VMEM((nplanes, halo, pitch), BF16),
            pltpu.VMEM((nplanes, halo, pitch), BF16),
            pltpu.VMEM((reach, 3, chunk, cols), BF16),
            pltpu.VMEM((reach, 3, chunk, cols), BF16),
            pltpu.VMEM((reach, 3, chunk, cols), BF16),
            pltpu.VMEM((reach, 3, chunk, cols), BF16),
            pltpu.VMEM((3, chunk, cols), BF16),
            pltpu.VMEM((3, chunk, cols), BF16),
            pltpu.VMEM((n, chunk, cols), BF16),
            sem((reach, 3)),
            sem((reach, 3)),
            sem((reach, 3)),
            sem((reach, 3)),
            sem,
            sem,
            sem((3,)),
            sem((3,)),
            sem((2,)),
            sem((2,)),
            sem((reach, 3)),
            sem((reach, 3)),
            sem((reach, 3)),
            sem((reach, 3)),
        ],
        compiler_params=pltpu.CompilerParams(
            collective_id=0, has_side_effects=True, vmem_limit_bytes=40 * 1024 * 1024
        ),
    )(planes.reshape(nplanes, rad, pitch), own, cross, ana, syn, rot)
    return out[:nrows].reshape(1, inst, fields, srows, pitch)


def solution(mesh):
    placed = (P("row", None, None, "span", "pitch"), P("span", None), P(), P(), P())
    return jax.shard_map(
        body, mesh=mesh, in_specs=placed,
        out_specs=P("row", None, None, "span", "pitch"), check_vma=False)
```

```python
import functools
import math

import jax
import jax.numpy as jnp
from jax import lax
from jax.experimental import pallas as pl
from jax.experimental.pallas import tpu as pltpu
from jax.sharding import PartitionSpec as P

BAND = 192
SUBS = 1
LAG = 2
MESH = pl.DeviceIdType.MESH
F32 = jnp.float32
BF16 = jnp.bfloat16


def nt_dot(a, b):
    return lax.dot_general(a, b, (((1,), (1,)), ((), ())), preferred_element_type=F32)


def nn_dot(a, b):
    return lax.dot_general(a, b, (((1,), (0,)), ((), ())), preferred_element_type=F32)


def wrapped(value, size):
    if size & (size - 1) == 0:
        return value & (size - 1)
    return jnp.mod(value, size)


def kernel(
    n, rows_n, chunk, subs, halo, half, srows,
    x_hbm, w_hbm, start_hbm, blade_hbm, order_hbm, out_hbm,
    x_ref, w_ref, start_ref, blade_ref, order_ref, out_ref, band_t, ana_ref, syn_ref, rot_ref,
    part, xsend, xrecv, sb_r, rb_r, sb_l, rb_l, sums, from_roots, gath,
    s_sr, s_rr, s_sl, s_rl, s_xs, s_xr, e_s, e_r, g_s, g_r, a_sr, a_rr, a_sl, a_rl, s_in, s_out, token,
):
    planes, rad, _ = x_ref.shape
    width = 128
    sub = chunk // subs
    reach = (n - 2) // 6
    far = 2 * reach + 1
    z = lax.axis_index("pitch")
    g = lax.axis_index("row")
    h = lax.axis_index("span")
    other = 1 - h
    partner = lax.rem(g + rows_n // 2, rows_n)

    def at(d):
        return lax.rem(z + (d + n), n)

    right, left = at(1), at(-1)
    offsets = (far, -far, 0)

    barrier = pltpu.get_barrier_semaphore()
    pace = (reach + 1) // 2
    ahead, behind = at(pace), at(-pace)
    peers = [{"pitch": left}, {"pitch": right}, {"span": other}, {"row": partner}]
    peers += [{"pitch": ahead}, {"pitch": behind}]
    for where in peers:
        pl.semaphore_signal(barrier, inc=1, device_id=where, device_id_type=MESH)

    x_in = pltpu.make_async_copy(x_hbm, x_ref, s_in.at[0])
    w_in = pltpu.make_async_copy(w_hbm, w_ref, s_in.at[1])
    start_in = pltpu.make_async_copy(start_hbm, start_ref, s_in.at[2])
    blade_in = pltpu.make_async_copy(blade_hbm, blade_ref, s_in.at[3])
    order_in = pltpu.make_async_copy(order_hbm, order_ref, s_in.at[4])
    blade_in.start()
    order_in.start()
    start_in.start()
    w_in.start()
    x_in.start()

    harm = order_ref.shape[1]
    blade_in.wait()
    order_in.wait()
    pitch = x_ref.shape[2]
    total_pitch = pitch * n
    wave_row = order_ref[0:1, :] * blade_ref[0] + order_ref[1:2, :] * blade_ref[1]
    wave = jnp.broadcast_to(wave_row.astype(F32), (128, harm)).T.astype(jnp.int32)
    spot = z * pitch + lax.broadcasted_iota(jnp.int32, (harm, pitch), 1)
    turns = wrapped(spot * wave, total_pitch)
    angle = 2.0 * math.pi / total_pitch * turns.astype(F32)
    both = jnp.concatenate([jnp.cos(angle), jnp.sin(angle)], axis=0)
    ana_ref[...] = (both * math.sqrt(2.0 / total_pitch)).astype(BF16)
    syn_ref[...] = (both * (1.0 / math.sqrt(harm))).astype(BF16)

    inst = planes // half
    moment = partner * inst + lax.broadcasted_iota(jnp.int32, (harm, 128), 1)
    steps = (wave * moment).astype(F32)
    period = (rows_n * inst * blade_ref[0]).astype(F32)
    left_over = steps - jnp.floor(steps / period) * period
    left_over = jnp.where(left_over < 0.0, left_over + period, left_over)
    left_over = jnp.where(left_over >= period, left_over - period, left_over)
    theta = 2.0 * math.pi * left_over / period
    cos_t, sin_t = jnp.cos(theta), jnp.sin(theta)
    rot_ref[0] = jnp.concatenate([cos_t, cos_t], axis=0).T
    rot_ref[1] = jnp.concatenate([-sin_t, sin_t], axis=0).T

    w_in.wait()
    start_in.wait()
    block = 128

    def band_rows(r, c):
        at_r = pl.ds(pl.multiple_of(r * block, block), block)
        rows = h * rad + r * block + lax.broadcasted_iota(jnp.int32, (block, w_ref.shape[1]), 0)
        begin = start_ref[...].reshape(1, w_ref.shape[1])
        inb = (rows >= begin) & (rows < begin + BAND)
        kept = jnp.where(inb, w_ref[at_r, :].astype(F32), 0.0)
        band_t[:, at_r] = kept.T.astype(BF16)
        return c

    lax.fori_loop(0, rad // block, band_rows, 0)
    x_in.wait()

    cols0 = (rad - width) * (1 - h)
    cross = band_t[pl.ds(pl.multiple_of(srows - halo * h, 16), halo), pl.ds(pl.multiple_of(cols0, 128), width)]

    def cross_plane(k, c):
        xk = x_ref[k, pl.ds(pl.multiple_of(cols0, 128), width), :]
        xsend[k] = nn_dot(cross, xk).astype(BF16)
        return c

    lax.fori_loop(0, planes, cross_plane, 0)

    pl.semaphore_wait(barrier, len(peers))

    def remote(src, dst, send, recv, where):
        return pltpu.make_async_remote_copy(
            src_ref=src, dst_ref=dst, send_sem=send, recv_sem=recv, device_id=where, device_id_type=MESH
        )

    xcopy = remote(xsend, xrecv, s_xs, s_xr, {"span": other})
    xcopy.start()

    def pass_on(k):
        for where in (ahead, behind):
            pl.semaphore_signal(token.at[k], inc=1, device_id={"pitch": where}, device_id_type=MESH)

    pass_on(0)

    ana = ana_ref[...]

    def own_plane(k, c):
        own = band_t[pl.ds(pl.multiple_of(h * srows, 16), srows), :]
        mk = nn_dot(own, x_ref[k]).astype(BF16)
        part[pl.ds(pl.multiple_of(k * srows, 16), srows), :] = nt_dot(mk, ana)
        return c

    lax.fori_loop(0, planes, own_plane, 0)
    tail = part.shape[0] - planes * srows
    if tail:
        part[planes * srows :, :] = jnp.zeros((tail, part.shape[1]), F32)
    pl.semaphore_wait(token.at[0], 2)
    pass_on(1)
    xcopy.wait_recv()
    b0 = (srows - halo) * (1 - h)

    def add_plane(k, c):
        rows = pl.ds(pl.multiple_of(k * srows + b0, 16), halo)
        part[rows, :] = part[rows, :] + nt_dot(xrecv[k], ana)
        return c

    lax.fori_loop(0, planes, add_plane, 0)

    pl.semaphore_wait(token.at[1], 2)

    def rows_of(c, j):
        return pl.ds(pl.multiple_of(c * chunk + j * sub, 16), sub)

    def send_r(s, k, j):
        return remote(
            sb_r.at[s, k, j], rb_r.at[s, k, j], s_sr.at[s, k, j], s_rr.at[s, k, j], {"pitch": right})

    def send_l(s, k, j):
        return remote(
            sb_l.at[s, k, j], rb_l.at[s, k, j], s_sl.at[s, k, j], s_rl.at[s, k, j], {"pitch": left})

    def first_r(k):
        return 1 if k == 1 else 0

    for s in range(reach):
        for k, off in enumerate(offsets):
            for j in range(subs):
                if s >= first_r(k):
                    value = part[rows_of(at(reach - s - off), j), :]
                    if s > first_r(k):
                        send_r(s - 1, k, j).wait_recv()
                        value = value + rb_r[s - 1, k, j].astype(F32)
                    sb_r[s, k, j] = value.astype(BF16)
                    send_r(s, k, j).start()
                value = part[rows_of(at(s - reach - off), j), :]
                if s > 0:
                    send_l(s - 1, k, j).wait_recv()
                    value = value + rb_l[s - 1, k, j].astype(F32)
                sb_l[s, k, j] = value.astype(BF16)
                send_l(s, k, j).start()

    def to_owner(k, j):
        where = {"row": partner, "pitch": at(-offsets[k])}
        return remote(sums.at[k, j], from_roots.at[k, j], e_s.at[k, j], e_r.at[k, j], where)

    for k, off in enumerate(offsets):
        for j in range(subs):
            value = part[rows_of(at(-off), j), :]
            send_l(reach - 1, k, j).wait_recv()
            value = value + rb_l[reach - 1, k, j].astype(F32)
            if reach - 1 >= first_r(k):
                send_r(reach - 1, k, j).wait_recv()
                value = value + rb_r[reach - 1, k, j].astype(F32)
            sums[k, j] = value.astype(BF16)
            to_owner(k, j).start()

    def to_root(k, j, incoming=False):
        c = gath.at[at(-offsets[k]), j] if incoming else gath.at[z, j]
        return remote(c, c, g_s.at[k, j], g_r.at[k, j], {"pitch": at(offsets[k])})

    def fwd_r(s, k, j, incoming=False):
        c = gath.at[at(-s - (1 if incoming else 0) - offsets[k]), j]
        return remote(c, c, a_sr.at[s, k, j], a_rr.at[s, k, j], {"pitch": right})

    def fwd_l(s, k, j, incoming=False):
        c = gath.at[at(s + (1 if incoming else 0) - offsets[k]), j]
        return remote(c, c, a_sl.at[s, k, j], a_rl.at[s, k, j], {"pitch": left})

    def last_l(k):
        return reach - 2 if k == 1 else reach - 1

    for j in range(subs):
        for k in (2, 0, 1):
            to_owner(k, j).wait_recv()
        total = from_roots[2, j].astype(F32) + from_roots[0, j].astype(F32) + from_roots[1, j].astype(F32)
        place = z * chunk + j * sub + lax.broadcasted_iota(jnp.int32, total.shape, 0)
        first = place < half * srows
        cosine = jnp.where(first, rot_ref[0, 0:1, :], rot_ref[0, 1:2, :])
        sine = jnp.where(first, rot_ref[1, 0:1, :], rot_ref[1, 1:2, :])
        swapped = pltpu.roll(total, total.shape[1] // 2, 1)
        gath[z, j] = (total * cosine + swapped * sine).astype(BF16)
        to_root(0, j).start()
        to_root(1, j).start()
        fwd_r(0, 2, j).start()
        fwd_l(0, 2, j).start()

    syn = syn_ref[...]

    def written(c):
        rows = pl.ds(pl.multiple_of(c * chunk, 16), chunk)
        return pltpu.make_async_copy(out_ref.at[rows], out_hbm.at[rows], s_out.at[c])

    def emit(c):
        for j in range(subs):
            out_ref[rows_of(c, j), :] = nn_dot(gath[c, j], syn).astype(BF16)
        written(c).start()

    emit(z)

    def take(k, s):
        ready = []
        if s == 0:
            for j in range(subs):
                to_root(k, j, True).wait_recv()
                fwd_r(0, k, j).start()
                if last_l(k) >= 0:
                    fwd_l(0, k, j).start()
            ready.append(at(-offsets[k]))
        else:
            for j in range(subs):
                fwd_r(s - 1, k, j, True).wait_recv()
                if s < reach:
                    fwd_r(s, k, j).start()
                if s - 1 <= last_l(k):
                    fwd_l(s - 1, k, j, True).wait_recv()
                    if s <= last_l(k):
                        fwd_l(s, k, j).start()
            ready.append(at(-s - offsets[k]))
            if s - 1 <= last_l(k):
                ready.append(at(s - offsets[k]))
        return ready

    lag = min(LAG, reach)
    for t in range(1, reach + lag + 1):
        ready = []
        if t <= reach:
            ready += take(2, t)
        if t >= lag:
            ready += take(0, t - lag)
            ready += take(1, t - lag)
        for c in ready:
            emit(c)

    xcopy.wait_send()
    for k in range(3):
        for j in range(subs):
            to_owner(k, j).wait_send()
            if k < 2:
                to_root(k, j).wait_send()
            for s in range(reach):
                if s >= first_r(k):
                    send_r(s, k, j).wait_send()
                send_l(s, k, j).wait_send()
                fwd_r(s, k, j).wait_send()
                if s <= last_l(k):
                    fwd_l(s, k, j).wait_send()

    def finish(c, carry):
        written(c).wait()
        return carry

    lax.fori_loop(0, n, finish, 0)


def body(outlet, remap_weight, band_start, blade_counts, mode_orders):
    row_count = lax.axis_size("row")
    n = lax.axis_size("pitch")
    planes = outlet[0]
    inst, fields, rad, pitch = planes.shape
    harm = mode_orders.shape[0]
    cols = 2 * harm
    stator = remap_weight.shape[1]
    srows = stator // 2
    nplanes = inst * fields
    halo = 112
    nrows = nplanes * srows
    chunk = -(-nrows // (n * 16)) * 16
    subs = SUBS if chunk % (16 * SUBS) == 0 else 1
    sub = chunk // subs
    reach = (n - 2) // 6
    sem = pltpu.SemaphoreType.DMA
    vm = pl.BlockSpec(memory_space=pltpu.VMEM)
    out = pl.pallas_call(
        functools.partial(kernel, n, row_count, chunk, subs, halo, fields, srows),
        out_shape=jax.ShapeDtypeStruct((n * chunk, pitch), BF16),
        in_specs=[pl.BlockSpec(memory_space=pltpu.HBM)] * 5,
        out_specs=pl.BlockSpec(memory_space=pltpu.HBM),
        scratch_shapes=[
            pltpu.VMEM((nplanes, rad, pitch), BF16),
            pltpu.VMEM((rad, stator), BF16),
            pltpu.VMEM((stator,), jnp.int32),
            pltpu.SMEM((2,), jnp.int32),
            pltpu.VMEM((2, harm), jnp.int32),
            pltpu.VMEM((n * chunk, pitch), BF16),
            pltpu.VMEM((stator, rad), BF16),
            pltpu.VMEM((cols, pitch), BF16),
            pltpu.VMEM((cols, pitch), BF16),
            pltpu.VMEM((2, 128, cols), F32),
            pltpu.VMEM((n * chunk, cols), F32),
            pltpu.VMEM((nplanes, halo, pitch), BF16),
            pltpu.VMEM((nplanes, halo, pitch), BF16),
            pltpu.VMEM((reach, 3, subs, sub, cols), BF16),
            pltpu.VMEM((reach, 3, subs, sub, cols), BF16),
            pltpu.VMEM((reach, 3, subs, sub, cols), BF16),
            pltpu.VMEM((reach, 3, subs, sub, cols), BF16),
            pltpu.VMEM((3, subs, sub, cols), BF16),
            pltpu.VMEM((3, subs, sub, cols), BF16),
            pltpu.VMEM((n, subs, sub, cols), BF16),
            sem((reach, 3, subs)),
            sem((reach, 3, subs)),
            sem((reach, 3, subs)),
            sem((reach, 3, subs)),
            sem,
            sem,
            sem((3, subs)),
            sem((3, subs)),
            sem((2, subs)),
            sem((2, subs)),
            sem((reach, 3, subs)),
            sem((reach, 3, subs)),
            sem((reach, 3, subs)),
            sem((reach, 3, subs)),
            sem((5,)),
            sem((n,)),
            pltpu.SemaphoreType.REGULAR((2,)),
        ],
        compiler_params=pltpu.CompilerParams(
            collective_id=0, has_side_effects=True, vmem_limit_bytes=63 * 1024 * 1024
        ),
    )(
        planes.reshape(nplanes, rad, pitch),
        remap_weight,
        band_start,
        blade_counts,
        mode_orders.T,
    )
    return out[:nrows].reshape(1, inst, fields, srows, pitch)


def solution(mesh):
    placed = (P("row", None, None, "span", "pitch"), P("span", None), P(), P(), P())
    return jax.shard_map(
        body, mesh=mesh, in_specs=placed,
        out_specs=P("row", None, None, "span", "pitch"), check_vma=False)
```
